32 devices in a mesh: group: 2 (over x), tm: 16 (over z, y, core).
Axes of the slice: x: 2, y: 2, z: 4, core: 2. Of those that a mesh axis runs over, the one named last changes fastest.
Arguments:
- records: float32 [256, 262144], P('group', 'tm'), parts along dimension 0, may hold values from -6 to 6
- labels: int32 [256], P('group'), parts along dimension 0, may hold values from 0 to 1
- first_weight: bfloat16 [131072, 1024], P('tm'), may hold values from -0.015625 to 0.015625
- first_bias: float32 [1024], replicated, may hold values from -3 to 3
- second_weight: float32 [1024], replicated, may hold values from -0.1875 to 0.1875
- second_bias: float32 [1], replicated, may hold values from -3 to 3
Outputs:
- loss: float32 [2], P('group'), parts along dimension 0
- grad_first: float32 [262144, 1024], P(('group', 'tm')), parts along dimension 0
- grad_bias: float32 [2048], P('group'), parts along dimension 0
- grad_second: float32 [2048], P('group'), parts along dimension 0
- grad_out_bias: float32 [2], P('group'), parts along dimension 0
The draws below stay inside these ranges and needn't reach their ends.
There are 2 independent parts, one for each index of `group`. The reference program is written for one: setup_inputs(seed, part) draws one part's arguments, and reference() takes and returns one part's arrays. A program takes and returns all parts, laid end to end along the dimension named above; an argument that names none is the same for every part. Nothing has to cross between parts.
All inputs are finite; a program needn't handle non-finite values.
Results may differ from the reference program's by a relative error of at most 0.0079.
Values may be sent and summed in bfloat16 or wider, within the bound.
No kernel may reach another device: no remote copies, remote signals or barrier semaphores. Data moves between devices by JAX's collectives and lax.ppermute only.
A program may use at most 192 MiB of HBM per device.

```python
import math
import jax
import jax.numpy as jnp
from jax import lax

N1 = 512
N2 = 512
HID = 1024
R = 128
L = 262144
F = 131072


def set_ends(drawn, own_key, least, high):
    dims = drawn.shape
    spot = [jax.random.randint(jax.random.fold_in(own_key, axis), (), 0, dims[axis]) for axis in range(len(dims))]
    drawn = drawn.at[tuple(spot)].set(least)
    longest = dims.index(max(dims))
    spot[longest] = (spot[longest] + 1) % dims[longest]
    return drawn.at[tuple(spot)].set(high)


def block_levels(stream_key, dims, cuts, least, high):
    level = 1.0
    for position, blocks in cuts:
        draws = jax.random.uniform(jax.random.fold_in(jax.random.fold_in(stream_key, 6), position), (blocks,), jnp.float32, least / len(cuts), high / len(cuts))
        level = level * jnp.repeat(jnp.exp(draws), dims[position] // blocks).reshape((-1,) + (1,) * (len(dims) - 1 - position))
    return level


def bell_draw(rng, extent, scale, most, shards=(), held_as=jnp.bfloat16):
    gain = block_levels(rng, extent, shards, -0.22, 0.18) if shards else 1.0
    drawn = jax.random.normal(rng, extent, jnp.float32) * scale * gain
    return jnp.minimum(jnp.maximum(drawn, -most), most).astype(held_as)


def setup_inputs(seed: int = 0, part: int = 0) -> dict:
    seeds = jax.random.split(jax.random.key(seed), 7)
    part_keys = jax.random.split(jax.random.fold_in(seeds[6], part), 7)
    return {
        "records": bell_draw(part_keys[0], (R, L), 1.0, 6.0, ((1, 16),), jnp.float32),
        "labels": set_ends(jax.random.randint(part_keys[1], (R,), 0, 2), jax.random.fold_in(part_keys[1], 1), 0, 1).astype(jnp.int32),
        "first_weight": bell_draw(seeds[2], (F, HID), F ** -0.5, 0.015625, ((0, 16),)),
        "first_bias": bell_draw(seeds[3], (HID,), 0.5, 3.0, (), jnp.float32),
        "second_weight": bell_draw(seeds[4], (HID,), HID ** -0.5, 0.1875, (), jnp.float32),
        "second_bias": bell_draw(seeds[5], (1,), 0.5, 3.0, (), jnp.float32),
    }


def first_table(count):
    rows = jnp.arange(count, dtype=jnp.int32)[:, None]
    cols = jnp.arange(count, dtype=jnp.int32)[None, :]
    angle = 2.0 * math.pi / count * (rows * cols % count).astype(jnp.float32)
    scale = 1.0 / math.sqrt(count)
    return jnp.concatenate([jnp.cos(angle) * scale, -jnp.sin(angle) * scale], 0).astype(jnp.bfloat16)

def second_table(count):
    rows = jnp.arange(count, dtype=jnp.int32)[:, None]
    cols = jnp.arange(count // 2, dtype=jnp.int32)[None, :]
    angle = 2.0 * math.pi / count * (rows * cols % count).astype(jnp.float32)
    scale = 1.0 / math.sqrt(count)
    cosine = jnp.cos(angle) * scale
    sine = jnp.sin(angle) * scale
    upper = jnp.concatenate([cosine, -sine], 1)
    lower = jnp.concatenate([sine, cosine], 1)
    return jnp.concatenate([upper, lower], 0).astype(jnp.bfloat16)

def reference(records, labels, first_weight, first_bias, second_weight, second_bias):
    table_one = first_table(N2)
    table_two = second_table(N1)
    slow = jnp.arange(N2, dtype=jnp.int32)[:, None]
    fast = jnp.arange(N1, dtype=jnp.int32)[None, :]
    phase = 2.0 * math.pi / L * (slow * fast % L).astype(jnp.float32)
    cosine = jnp.cos(phase)
    sine = jnp.sin(phase)

    def spectrum(record):
        block = record.astype(jnp.bfloat16).reshape(N2, N1)
        partial_value = jnp.dot(table_one, block, preferred_element_type=jnp.float32)
        real_part = partial_value[:N2]
        imag_part = partial_value[N2:]
        twisted_re = real_part * cosine + imag_part * sine
        twisted_im = imag_part * cosine - real_part * sine
        twisted = jnp.concatenate([twisted_re, twisted_im], 1).astype(jnp.bfloat16)
        bins = jnp.dot(twisted, table_two, preferred_element_type=jnp.float32)
        power = bins[:, :N1 // 2] ** 2 + bins[:, N1 // 2:] ** 2
        return jnp.log(1.0 + power).astype(jnp.bfloat16).reshape(F)
    features = lax.map(spectrum, records)
    target = labels.astype(jnp.float32)
    pre = jnp.dot(features, first_weight, preferred_element_type=jnp.float32) + first_bias[None, :]
    gate = jax.nn.sigmoid(pre)
    hidden = pre * gate
    logit = lax.optimization_barrier(jnp.sum(hidden * second_weight[None, :], 1)) + second_bias[0]
    loss = jnp.mean(jnp.log(1.0 + jnp.exp(logit)) - target * logit).reshape(1)
    dlogit = jax.nn.sigmoid(logit) - target
    dpre = (dlogit[:, None] * second_weight[None, :] * gate * (1.0 + pre * (1.0 - gate))).astype(jnp.bfloat16)
    grad_first = lax.dot_general(features, dpre, (((0,), (0,)), ((), ())), preferred_element_type=jnp.float32)
    grad_bias = lax.optimization_barrier(jnp.sum(dpre.astype(jnp.float32), 0))
    grad_second = lax.optimization_barrier(jnp.sum(hidden * dlogit[:, None], 0))
    grad_out_bias = jnp.sum(dlogit).reshape(1)
    return (loss, grad_first, grad_bias, grad_second, grad_out_bias)
```

```python
import functools
import math

import jax
import jax.numpy as jnp
import numpy as np
from jax import lax
from jax.experimental import pallas as pl
from jax.experimental.pallas import tpu as pltpu
from jax.sharding import PartitionSpec as P

N1 = 512
N2 = 512
HALF = N1 // 2
LANES = 128
ROW_BLOCK = 8
VMEM_LIMIT = 50 * 2**20


def tables():
    rows = np.arange(N2)[:, None]
    cols = np.arange(N2)[None, :]
    angle = 2.0 * math.pi / N2 * (rows * cols % N2)
    scale = 1.0 / math.sqrt(N2)
    one = np.concatenate([np.cos(angle) * scale, -np.sin(angle) * scale], 0)
    angle = 2.0 * math.pi / N1 * (np.arange(N1)[:, None] * np.arange(HALF)[None, :] % N1)
    scale = 1.0 / math.sqrt(N1)
    cosine, sine = np.cos(angle) * scale, np.sin(angle) * scale
    two = np.concatenate(
        [np.concatenate([cosine, -sine], 1), np.concatenate([sine, cosine], 1)], 0
    )
    total = N1 * N2
    phase = 2.0 * math.pi / total * (np.arange(N2)[:, None] * np.arange(N1)[None, :] % total)
    return (
        jnp.asarray(one.astype(np.float32), jnp.bfloat16),
        jnp.asarray(np.cos(phase).astype(np.float32)),
        jnp.asarray(np.sin(phase).astype(np.float32)),
        jnp.asarray(two.astype(np.float32), jnp.bfloat16),
    )


def prepare_kernel(x_ref, o_ref):
    slow = o_ref.shape[1]
    pieces = N1 // LANES
    for rec in range(ROW_BLOCK):
        for piece in range(pieces):
            rows = pl.ds(piece * ROW_BLOCK + rec, slow, stride=pieces * ROW_BLOCK)
            o_ref[rec, :, piece * LANES : (piece + 1) * LANES] = x_ref[0, rows, :].astype(
                jnp.bfloat16
            )


def prepare(view, first_row, rows, slow):
    first = first_row // ROW_BLOCK
    return pl.pallas_call(
        prepare_kernel,
        grid=(rows // ROW_BLOCK,),
        in_specs=[pl.BlockSpec((1, view.shape[1], LANES), lambda i: (i + first, 0, 0))],
        out_specs=pl.BlockSpec((ROW_BLOCK, slow, N1), lambda i: (i, 0, 0)),
        out_shape=jax.ShapeDtypeStruct((rows, slow, N1), jnp.bfloat16),
        cost_estimate=pl.CostEstimate(
            flops=rows * slow * N1, bytes_accessed=rows * slow * N1 * 6, transcendentals=0
        ),
        name="prepare",
    )(view)


def spectrum_kernel(x_ref, one_ref, cos_ref, sin_ref, two_ref, o_ref, *, block):
    parts, _, slow, _ = o_ref.shape
    data = x_ref[...].reshape(N2, N1)
    for start in range(0, N2, block):
        rows = slice(start, start + block)
        real = jnp.dot(one_ref[rows, :], data, preferred_element_type=jnp.float32)
        imag = jnp.dot(
            one_ref[N2 + start : N2 + start + block, :], data, preferred_element_type=jnp.float32
        )
        cosine = cos_ref[rows, :]
        sine = sin_ref[rows, :]
        twisted_re = (real * cosine + imag * sine).astype(jnp.bfloat16)
        twisted_im = (imag * cosine - real * sine).astype(jnp.bfloat16)
        bins = jnp.dot(twisted_re, two_ref[:N1, :], preferred_element_type=jnp.float32)
        bins += jnp.dot(twisted_im, two_ref[N1:, :], preferred_element_type=jnp.float32)
        power = bins[:, :HALF] ** 2 + bins[:, HALF:] ** 2
        feats = jnp.log(1.0 + power).astype(jnp.bfloat16)
        if parts == 1:
            o_ref[0, 0, rows, :] = feats
        else:
            o_ref[start // slow : (start + block) // slow, 0] = feats.reshape(
                block // slow, slow, HALF
            )


def spectrum(blocks, consts):
    parts, count, slow, _ = blocks.shape
    whole = lambda a: pl.BlockSpec(a.shape, lambda i: (0, 0))
    return pl.pallas_call(
        functools.partial(spectrum_kernel, block=max(128, slow)),
        grid=(count,),
        in_specs=[pl.BlockSpec((parts, 1, slow, N1), lambda i: (0, i, 0, 0))]
        + [whole(a) for a in consts],
        out_specs=pl.BlockSpec((parts, 1, slow, HALF), lambda i: (0, i, 0, 0)),
        out_shape=jax.ShapeDtypeStruct((parts, count, slow, HALF), jnp.bfloat16),
        compiler_params=pltpu.CompilerParams(vmem_limit_bytes=VMEM_LIMIT),
        cost_estimate=pl.CostEstimate(
            flops=count * 8 * N1 * N2 * N2,
            bytes_accessed=count * N1 * N2 * 3 + 4 * 2**20,
            transcendentals=count * N2 * HALF,
        ),
        name="spectrum",
    )(blocks, *consts)


def sum_over(value, devices):
    bit = 1
    while bit < devices:
        pairs = [(i, i ^ bit) for i in range(devices)]
        value = value + lax.ppermute(value, "tm", pairs)
        bit *= 2
    return value


def on_device(records, labels, first_weight, first_bias, second_weight, second_bias):
    devices = lax.axis_size("tm")
    count, local = records.shape
    slow = local // N1
    each = count // devices
    chunks = {8: (4,4)}.get(each, (each,))
    aligned = slow % 16 == 0
    consts = tables()
    pieces = N1 // LANES
    view = (
        records.reshape(count // ROW_BLOCK, ROW_BLOCK, slow, pieces, LANES)
        .transpose(0, 2, 3, 1, 4)
        .reshape(count // ROW_BLOCK, slow * pieces * ROW_BLOCK, LANES)
    )

    feature_chunks, pre_chunks = [], []
    row = 0
    for size in chunks:
        rows = size * devices
        mine = prepare(view, row, rows, slow).reshape(devices, size, slow, N1)
        blocks = lax.all_to_all(mine, "tm", split_axis=0, concat_axis=0, tiled=True)
        if not aligned:
            blocks = blocks.transpose(1, 0, 2, 3).reshape(1, size, N2, N1)
        feats = spectrum(blocks, consts)
        if not aligned:
            feats = feats.reshape(size, devices, slow, HALF).transpose(1, 0, 2, 3)
        feats = lax.all_to_all(feats, "tm", split_axis=0, concat_axis=0, tiled=True)
        feats = feats.reshape(rows, slow * HALF)
        feature_chunks.append(feats)
        partial_sums = jnp.dot(feats, first_weight, preferred_element_type=jnp.float32)
        pre_chunks.append(sum_over(partial_sums, devices))
        row += rows
    features = jnp.concatenate(feature_chunks, 0)
    pre = jnp.concatenate(pre_chunks, 0) + first_bias[None, :]

    target = labels.astype(jnp.float32)
    gate = jax.nn.sigmoid(pre)
    hidden = pre * gate
    logit = jnp.sum(hidden * second_weight[None, :], 1) + second_bias[0]
    dlogit = jax.nn.sigmoid(logit) - target
    dpre = (dlogit[:, None] * second_weight[None, :] * gate * (1.0 + pre * (1.0 - gate))).astype(
        jnp.bfloat16
    )
    grad_first = lax.dot_general(
        features, dpre, (((0,), (0,)), ((), ())), preferred_element_type=jnp.float32
    )
    grad_bias = jnp.sum(dpre.astype(jnp.float32), 0)
    grad_second = jnp.sum(hidden * dlogit[:, None], 0)
    loss = jnp.mean(jnp.log(1.0 + jnp.exp(logit)) - target * logit).reshape(1)
    grad_out_bias = jnp.sum(dlogit).reshape(1)
    return (loss, grad_first, grad_bias, grad_second, grad_out_bias)


def solution(mesh):
    return jax.shard_map(
        on_device,
        mesh=mesh,
        in_specs=(P("group", "tm"), P("group"), P("tm", None), P(), P(), P()),
        out_specs=(P("group"), P(("group", "tm"), None), P("group"), P("group"), P("group")),
        check_vma=False,
    )
```

```python
import functools
import math

import jax
import jax.numpy as jnp
import numpy as np
from jax import lax
from jax.experimental import pallas as pl
from jax.experimental.pallas import tpu as pltpu
from jax.sharding import PartitionSpec as P

N1 = 512
N2 = 512
HALF = N1 // 2
LANES = 128
ROW_BLOCK = 8
VMEM_LIMIT = 50 * 2**20


def tables():
    rows = np.arange(N2)[:, None]
    cols = np.arange(N2)[None, :]
    angle = 2.0 * math.pi / N2 * (rows * cols % N2)
    scale = 1.0 / math.sqrt(N2)
    table = np.concatenate([np.cos(angle) * scale, -np.sin(angle) * scale], 0)
    total = N1 * N2
    slow = jnp.arange(N2, dtype=jnp.int32)[:, None]
    fast = jnp.arange(N1, dtype=jnp.int32)[None, :]
    phase = 2.0 * math.pi / total * (slow * fast % total).astype(jnp.float32)
    return jnp.asarray(table.astype(np.float32), jnp.bfloat16), jnp.cos(phase), jnp.sin(phase)


def prepare_kernel(*refs):
    *x_refs, o_ref = refs
    slow = o_ref.shape[1]
    step = math.gcd(slow, 16)
    for eight, x_ref in enumerate(x_refs):
        recs = slice(eight * ROW_BLOCK, (eight + 1) * ROW_BLOCK)
        for start in range(0, slow, step):
            rows = slice(start, start + step)
            for piece in range(N1 // LANES):
                value = x_ref[0, rows, piece].astype(jnp.bfloat16)
                o_ref[recs, rows, piece * LANES : (piece + 1) * LANES] = jnp.swapaxes(value, 0, 1)


def prepare(view, first_row, rows, slow):
    first = first_row // ROW_BLOCK
    eights = rows // ROW_BLOCK
    streams = next(s for s in (4, 3, 5, 2, 1) if eights % s == 0)
    block = (1,) + view.shape[1:]
    spec = lambda s: pl.BlockSpec(block, lambda i: (i * streams + s + first, 0, 0, 0, 0))
    return pl.pallas_call(
        prepare_kernel,
        grid=(eights // streams,),
        in_specs=[spec(s) for s in range(streams)],
        out_specs=pl.BlockSpec((streams * ROW_BLOCK, slow, N1), lambda i: (i, 0, 0)),
        out_shape=jax.ShapeDtypeStruct((rows, slow, N1), jnp.bfloat16),
        compiler_params=pltpu.CompilerParams(vmem_limit_bytes=VMEM_LIMIT),
        cost_estimate=pl.CostEstimate(
            flops=rows * slow * N1, bytes_accessed=rows * slow * N1 * 6, transcendentals=0
        ),
        name="prepare",
    )(*[view] * streams)


def spectrum_kernel(x_ref, table_ref, cos_ref, sin_ref, o_ref, *, block):
    parts, _, slow, _ = o_ref.shape
    data = x_ref[...].reshape(N2, N1)
    dot = functools.partial(jnp.dot, preferred_element_type=jnp.float32)
    for start in range(0, N2, block):
        rows = slice(start, start + block)
        real = dot(table_ref[rows, :], data)
        imag = dot(table_ref[N2 + start : N2 + start + block, :], data)
        cosine = cos_ref[rows, :]
        sine = sin_ref[rows, :]
        twisted_re = (real * cosine + imag * sine).astype(jnp.bfloat16)
        twisted_im = (imag * cosine - real * sine).astype(jnp.bfloat16)
        table_cos = table_ref[:N1, :HALF]
        minus_sin = table_ref[N1:, :HALF]
        bins_re = dot(twisted_re, table_cos) - dot(twisted_im, minus_sin)
        bins_im = dot(twisted_re, minus_sin) + dot(twisted_im, table_cos)
        feats = jnp.log(1.0 + (bins_re**2 + bins_im**2)).astype(jnp.bfloat16)
        if parts == 1:
            o_ref[0, 0, rows, :] = feats
        else:
            o_ref[start // slow : (start + block) // slow, 0] = feats.reshape(
                block // slow, slow, HALF
            )


def spectrum(blocks, consts):
    parts, count, slow, _ = blocks.shape
    whole = lambda a: pl.BlockSpec(a.shape, lambda i: (0, 0))
    return pl.pallas_call(
        functools.partial(spectrum_kernel, block=max(128, slow)),
        grid=(count,),
        in_specs=[pl.BlockSpec((parts, 1, slow, N1), lambda i: (0, i, 0, 0))]
        + [whole(a) for a in consts],
        out_specs=pl.BlockSpec((parts, 1, slow, HALF), lambda i: (0, i, 0, 0)),
        out_shape=jax.ShapeDtypeStruct((parts, count, slow, HALF), jnp.bfloat16),
        compiler_params=pltpu.CompilerParams(vmem_limit_bytes=VMEM_LIMIT),
        cost_estimate=pl.CostEstimate(
            flops=count * 8 * N1 * N2 * N2,
            bytes_accessed=count * N1 * N2 * 3 + 4 * 2**20,
            transcendentals=count * N2 * HALF,
        ),
        name="spectrum",
    )(blocks, *consts)


def exchange(value, bit, devices):
    return lax.ppermute(value, "tm", [(i, i ^ bit) for i in range(devices)])


def sum_over(value, devices):
    quarter = value.shape[1] // 4
    if devices % 4:
        bit = 1
        while bit < devices:
            value = value + exchange(value, bit, devices)
            bit *= 2
        return value
    me = lax.axis_index("tm") % 4
    part = [
        lax.dynamic_slice_in_dim(value, (me ^ k) * quarter, quarter, 1) for k in range(4)
    ]
    got = [exchange(part[k], k, devices) for k in range(1, 4)]
    own = (part[0] + got[0]) + (got[1] + got[2])
    if devices == 16:
        got = [exchange(own, 4 * k, devices) for k in range(1, 4)]
        own = (own + got[0]) + (got[1] + got[2])
    else:
        bit = 4
        while bit < devices:
            own = own + exchange(own, bit, devices)
            bit *= 2
    got = [own] + [exchange(own, k, devices) for k in range(1, 4)]
    odd = (me % 2) == 1
    high = me >= 2
    low_pair = [jnp.where(odd, got[1], got[0]), jnp.where(odd, got[0], got[1])]
    high_pair = [jnp.where(odd, got[3], got[2]), jnp.where(odd, got[2], got[3])]
    return jnp.concatenate(
        [jnp.where(high, h, l) for l, h in zip(low_pair, high_pair)]
        + [jnp.where(high, l, h) for l, h in zip(low_pair, high_pair)],
        1,
    )


def on_device(records, labels, first_weight, first_bias, second_weight, second_bias):
    devices = lax.axis_size("tm")
    count, local = records.shape
    slow = local // N1
    each = count // devices
    chunks = {8: (3, 5)}.get(each, (each,))
    aligned = slow % 16 == 0
    consts = tables()
    pieces = N1 // LANES
    view = (
        records.reshape(count // ROW_BLOCK, ROW_BLOCK, slow, pieces, LANES)
        .transpose(0, 2, 3, 1, 4)
    )

    feature_chunks, pre_chunks = [], []
    row = 0
    for size in chunks:
        rows = size * devices
        mine = prepare(view, row, rows, slow).reshape(devices, size, slow, N1)
        blocks = lax.all_to_all(mine, "tm", split_axis=0, concat_axis=0, tiled=True)
        if not aligned:
            blocks = blocks.transpose(1, 0, 2, 3).reshape(1, size, N2, N1)
        feats = spectrum(blocks, consts)
        if not aligned:
            feats = feats.reshape(size, devices, slow, HALF).transpose(1, 0, 2, 3)
        feats = lax.all_to_all(feats, "tm", split_axis=0, concat_axis=0, tiled=True)
        feats = feats.reshape(rows, slow * HALF)
        feature_chunks.append(feats)
        partial_sums = jnp.dot(feats, first_weight, preferred_element_type=jnp.float32)
        pre_chunks.append(sum_over(partial_sums, devices))
        row += rows
    features = jnp.concatenate(feature_chunks, 0)
    pre = jnp.concatenate(pre_chunks, 0) + first_bias[None, :]

    target = labels.astype(jnp.float32)
    gate = jax.nn.sigmoid(pre)
    hidden = pre * gate
    logit = jnp.sum(hidden * second_weight[None, :], 1) + second_bias[0]
    dlogit = jax.nn.sigmoid(logit) - target
    dpre = (dlogit[:, None] * second_weight[None, :] * gate * (1.0 + pre * (1.0 - gate))).astype(
        jnp.bfloat16
    )
    grad_first = lax.dot_general(
        features, dpre, (((0,), (0,)), ((), ())), preferred_element_type=jnp.float32
    )
    grad_bias = jnp.sum(dpre.astype(jnp.float32), 0)
    grad_second = jnp.sum(hidden * dlogit[:, None], 0)
    loss = jnp.mean(jnp.log(1.0 + jnp.exp(logit)) - target * logit).reshape(1)
    grad_out_bias = jnp.sum(dlogit).reshape(1)
    return (loss, grad_first, grad_bias, grad_second, grad_out_bias)


def solution(mesh):
    return jax.shard_map(
        on_device,
        mesh=mesh,
        in_specs=(P("group", "tm"), P("group"), P("tm", None), P(), P(), P()),
        out_specs=(P("group"), P(("group", "tm"), None), P("group"), P("group"), P("group")),
        check_vma=False,
    )
```

```python
import functools
import math

import jax
import jax.numpy as jnp
import numpy as np
from jax import lax
from jax.experimental import pallas as pl
from jax.experimental.pallas import tpu as pltpu
from jax.sharding import PartitionSpec as P

N1 = 512
N2 = 512
HALF = N1 // 2
LANES = 128
ROW_BLOCK = 8
VMEM_LIMIT = 50 * 2**20
PRODUCT_STEP = 512


def tables():
    rows = np.arange(N2)[:, None]
    cols = np.arange(N2)[None, :]
    angle = 2.0 * math.pi / N2 * (rows * cols % N2)
    scale = 1.0 / math.sqrt(N2)
    table = np.concatenate([np.cos(angle) * scale, -np.sin(angle) * scale], 0)
    total = N1 * N2
    slow = jnp.arange(N2, dtype=jnp.int32)[:, None]
    fast = jnp.arange(N1, dtype=jnp.int32)[None, :]
    phase = 2.0 * math.pi / total * (slow * fast % total).astype(jnp.float32)
    return jnp.asarray(table.astype(np.float32), jnp.bfloat16), jnp.cos(phase), jnp.sin(phase)


def prepare_kernel(*refs):
    *x_refs, o_ref = refs
    slow = o_ref.shape[1]
    step = math.gcd(slow, 16)
    for eight, x_ref in enumerate(x_refs):
        recs = slice(eight * ROW_BLOCK, (eight + 1) * ROW_BLOCK)
        for start in range(0, slow, step):
            rows = slice(start, start + step)
            for piece in range(N1 // LANES):
                value = x_ref[0, rows, piece].astype(jnp.bfloat16)
                o_ref[recs, rows, piece * LANES : (piece + 1) * LANES] = jnp.swapaxes(value, 0, 1)


def prepare(view, first_row, rows, slow):
    first = first_row // ROW_BLOCK
    eights = rows // ROW_BLOCK
    streams = next(s for s in (4, 3, 5, 2, 1) if eights % s == 0)
    block = (1,) + view.shape[1:]
    spec = lambda s: pl.BlockSpec(block, lambda i: (i * streams + s + first, 0, 0, 0, 0))
    return pl.pallas_call(
        prepare_kernel,
        grid=(eights // streams,),
        in_specs=[spec(s) for s in range(streams)],
        out_specs=pl.BlockSpec((streams * ROW_BLOCK, slow, N1), lambda i: (i, 0, 0)),
        out_shape=jax.ShapeDtypeStruct((rows, slow, N1), jnp.bfloat16),
        compiler_params=pltpu.CompilerParams(vmem_limit_bytes=VMEM_LIMIT),
        cost_estimate=pl.CostEstimate(
            flops=rows * slow * N1, bytes_accessed=rows * slow * N1 * 6, transcendentals=0
        ),
        name="prepare",
    )(*[view] * streams)


def spectrum_kernel(x_ref, table_ref, cos_ref, sin_ref, o_ref, *, block):
    parts, _, slow, _ = o_ref.shape
    data = x_ref[...].reshape(N2, N1)
    dot = functools.partial(jnp.dot, preferred_element_type=jnp.float32)
    for start in range(0, N2, block):
        rows = slice(start, start + block)
        real = dot(table_ref[rows, :], data)
        imag = dot(table_ref[N2 + start : N2 + start + block, :], data)
        cosine = cos_ref[rows, :]
        sine = sin_ref[rows, :]
        twisted_re = (real * cosine + imag * sine).astype(jnp.bfloat16)
        twisted_im = (imag * cosine - real * sine).astype(jnp.bfloat16)
        table_cos = table_ref[:N1, :HALF]
        minus_sin = table_ref[N1:, :HALF]
        bins_re = dot(twisted_re, table_cos) - dot(twisted_im, minus_sin)
        bins_im = dot(twisted_re, minus_sin) + dot(twisted_im, table_cos)
        feats = jnp.log(1.0 + (bins_re**2 + bins_im**2)).astype(jnp.bfloat16)
        if parts == 1:
            o_ref[0, 0, rows, :] = feats
        else:
            o_ref[start // slow : (start + block) // slow, 0] = feats.reshape(
                block // slow, slow, HALF
            )


def spectrum(blocks, consts):
    parts, count, slow, _ = blocks.shape
    whole = lambda a: pl.BlockSpec(a.shape, lambda i: (0, 0))
    return pl.pallas_call(
        functools.partial(spectrum_kernel, block=max(128, slow)),
        grid=(count,),
        in_specs=[pl.BlockSpec((parts, 1, slow, N1), lambda i: (0, i, 0, 0))]
        + [whole(a) for a in consts],
        out_specs=pl.BlockSpec((parts, 1, slow, HALF), lambda i: (0, i, 0, 0)),
        out_shape=jax.ShapeDtypeStruct((parts, count, slow, HALF), jnp.bfloat16),
        compiler_params=pltpu.CompilerParams(vmem_limit_bytes=VMEM_LIMIT),
        cost_estimate=pl.CostEstimate(
            flops=count * 8 * N1 * N2 * N2,
            bytes_accessed=count * N1 * N2 * 3 + 4 * 2**20,
            transcendentals=count * N2 * HALF,
        ),
        name="spectrum",
    )(blocks, *consts)


def gradient_kernel(*refs, block, slots):
    *feat_refs, dpre_ref, o_ref, buffer, sems = refs
    blocks = o_ref.shape[0] // block

    def copy(k):
        return pltpu.make_async_copy(
            buffer.at[k % slots], o_ref.at[pl.ds(k * block, block), :], sems.at[k % slots]
        )

    for k in range(blocks):
        if k >= slots:
            copy(k - slots).wait()
        feats = jnp.concatenate([ref[:, k * block : (k + 1) * block] for ref in feat_refs], 0)
        buffer[k % slots] = lax.dot_general(
            feats, dpre_ref[...], (((0,), (0,)), ((), ())), preferred_element_type=jnp.float32
        )
        copy(k).start()
    for k in range(max(0, blocks - slots), blocks):
        copy(k).wait()


def gradient(chunks, dpre):
    features, hid = chunks[0].shape[1], dpre.shape[1]
    block = min(256, features)
    slots = min(8, features // block)
    return pl.pallas_call(
        functools.partial(gradient_kernel, block=block, slots=slots),
        in_specs=[pl.BlockSpec(memory_space=pltpu.VMEM)] * (len(chunks) + 1),
        out_specs=pl.BlockSpec(memory_space=pl.ANY),
        out_shape=jax.ShapeDtypeStruct((features, hid), jnp.float32),
        scratch_shapes=[
            pltpu.VMEM((slots, block, hid), jnp.float32),
            pltpu.SemaphoreType.DMA((slots,)),
        ],
        compiler_params=pltpu.CompilerParams(vmem_limit_bytes=24 * 2**20),
        cost_estimate=pl.CostEstimate(
            flops=2 * features * hid * dpre.shape[0],
            bytes_accessed=features * hid * 4,
            transcendentals=0,
        ),
        name="gradient",
    )(*chunks, dpre)


def exchange(value, bit, devices):
    return lax.ppermute(value, "tm", [(i, i ^ bit) for i in range(devices)])


def product_kernel(feats_ref, weight_ref, o_ref, held_ref, sems, *, step):
    copies = []
    for k in range(weight_ref.shape[0] // step):
        rows = pl.ds(k * step, step)
        copies.append(
            pltpu.make_async_copy(weight_ref.at[rows, :], held_ref.at[rows, :], sems.at[k])
        )
        copies[-1].start()
    total = None
    for k, copy in enumerate(copies):
        copy.wait()
        rows = slice(k * step, (k + 1) * step)
        piece = jnp.dot(
            feats_ref[:, rows], held_ref[rows, :], preferred_element_type=jnp.float32
        )
        total = piece if total is None else total + piece
    o_ref[...] = total


def product(feats, weight):
    rows, (depth, hid) = feats.shape[0], weight.shape
    step = min(PRODUCT_STEP, depth)
    vmem = pl.BlockSpec(memory_space=pltpu.VMEM)
    return pl.pallas_call(
        functools.partial(product_kernel, step=step),
        in_specs=[vmem, pl.BlockSpec(memory_space=pl.ANY)],
        out_specs=vmem,
        out_shape=jax.ShapeDtypeStruct((rows, hid), jnp.float32),
        scratch_shapes=[
            pltpu.VMEM((depth, hid), weight.dtype),
            pltpu.SemaphoreType.DMA((depth // step,)),
        ],
        compiler_params=pltpu.CompilerParams(vmem_limit_bytes=49 * 2**20),
        cost_estimate=pl.CostEstimate(
            flops=2 * rows * weight.size, bytes_accessed=weight.size * 2, transcendentals=0
        ),
        name="product",
    )(feats, weight)


def sum_over(value, devices):
    quarter = value.shape[1] // 4
    if devices % 4:
        bit = 1
        while bit < devices:
            value = value + exchange(value, bit, devices)
            bit *= 2
        return value
    me = lax.axis_index("tm") % 4
    part = [
        lax.dynamic_slice_in_dim(value, (me ^ k) * quarter, quarter, 1) for k in range(4)
    ]
    got = [exchange(part[k], k, devices) for k in range(1, 4)]
    own = (part[0] + got[0]) + (got[1] + got[2])
    if devices == 16:
        got = [exchange(own, 4 * k, devices) for k in range(1, 4)]
        own = (own + got[0]) + (got[1] + got[2])
    else:
        bit = 4
        while bit < devices:
            own = own + exchange(own, bit, devices)
            bit *= 2
    got = [own] + [exchange(own, k, devices) for k in range(1, 4)]
    odd = (me % 2) == 1
    high = me >= 2
    low_pair = [jnp.where(odd, got[1], got[0]), jnp.where(odd, got[0], got[1])]
    high_pair = [jnp.where(odd, got[3], got[2]), jnp.where(odd, got[2], got[3])]
    return jnp.concatenate(
        [jnp.where(high, h, l) for l, h in zip(low_pair, high_pair)]
        + [jnp.where(high, l, h) for l, h in zip(low_pair, high_pair)],
        1,
    )


def on_device(records, labels, first_weight, first_bias, second_weight, second_bias):
    devices = lax.axis_size("tm")
    count, local = records.shape
    slow = local // N1
    each = count // devices
    chunks = {8: (3, 5)}.get(each, (each,))
    aligned = slow % 16 == 0
    consts = tables()
    pieces = N1 // LANES
    view = (
        records.reshape(count // ROW_BLOCK, ROW_BLOCK, slow, pieces, LANES)
        .transpose(0, 2, 3, 1, 4)
    )

    feature_chunks, pre_chunks = [], []
    row = 0
    for size in chunks:
        rows = size * devices
        mine = prepare(view, row, rows, slow).reshape(devices, size, slow, N1)
        blocks = lax.all_to_all(mine, "tm", split_axis=0, concat_axis=0, tiled=True)
        if not aligned:
            blocks = blocks.transpose(1, 0, 2, 3).reshape(1, size, N2, N1)
        feats = spectrum(blocks, consts)
        if not aligned:
            feats = feats.reshape(size, devices, slow, HALF).transpose(1, 0, 2, 3)
        feats = lax.all_to_all(feats, "tm", split_axis=0, concat_axis=0, tiled=True)
        feats = feats.reshape(rows, slow * HALF)
        feature_chunks.append(feats)
        partial_sums = product(feats, first_weight)
        pre_chunks.append(sum_over(partial_sums, devices))
        row += rows
    pre = jnp.concatenate(pre_chunks, 0) + first_bias[None, :]

    target = labels.astype(jnp.float32)
    gate = jax.nn.sigmoid(pre)
    hidden = pre * gate
    logit = jnp.sum(hidden * second_weight[None, :], 1) + second_bias[0]
    dlogit = jax.nn.sigmoid(logit) - target
    dpre = (dlogit[:, None] * second_weight[None, :] * gate * (1.0 + pre * (1.0 - gate))).astype(
        jnp.bfloat16
    )
    grad_first = gradient(feature_chunks, dpre)
    grad_bias = jnp.sum(dpre.astype(jnp.float32), 0)
    grad_second = jnp.sum(hidden * dlogit[:, None], 0)
    loss = jnp.mean(jnp.log(1.0 + jnp.exp(logit)) - target * logit).reshape(1)
    grad_out_bias = jnp.sum(dlogit).reshape(1)
    return (loss, grad_first, grad_bias, grad_second, grad_out_bias)


def solution(mesh):
    return jax.shard_map(
        on_device,
        mesh=mesh,
        in_specs=(P("group", "tm"), P("group"), P("tm", None), P(), P(), P()),
        out_specs=(P("group"), P(("group", "tm"), None), P("group"), P("group"), P("group")),
        check_vma=False,
    )
```

```python
import functools
import math

import jax
import jax.numpy as jnp
import numpy as np
from jax import lax
from jax.experimental import pallas as pl
from jax.experimental.pallas import tpu as pltpu
from jax.sharding import PartitionSpec as P

N1 = 512
N2 = 512
HALF = N1 // 2
LANES = 128
ROW_BLOCK = 8
VMEM_LIMIT = 50 * 2**20
PRODUCT_STEP = 512


def tables():
    rows = np.arange(N2)[:, None]
    cols = np.arange(N2)[None, :]
    angle = 2.0 * math.pi / N2 * (rows * cols % N2)
    scale = 1.0 / math.sqrt(N2)
    table = np.concatenate([np.cos(angle) * scale, -np.sin(angle) * scale], 0)
    total = N1 * N2
    slow = jnp.arange(N2, dtype=jnp.int32)[:, None]
    fast = jnp.arange(N1, dtype=jnp.int32)[None, :]
    phase = 2.0 * math.pi / total * (slow * fast % total).astype(jnp.float32)
    return jnp.asarray(table.astype(np.float32), jnp.bfloat16), jnp.cos(phase), jnp.sin(phase)


def prepare_kernel(*refs):
    *x_refs, o_ref = refs
    slow = o_ref.shape[1]
    step = math.gcd(slow, 16)
    for eight, x_ref in enumerate(x_refs):
        recs = slice(eight * ROW_BLOCK, (eight + 1) * ROW_BLOCK)
        for start in range(0, slow, step):
            rows = slice(start, start + step)
            for piece in range(N1 // LANES):
                value = x_ref[0, rows, piece].astype(jnp.bfloat16)
                o_ref[recs, rows, piece * LANES : (piece + 1) * LANES] = jnp.swapaxes(value, 0, 1)


def prepare(view, first_row, rows, slow):
    first = first_row // ROW_BLOCK
    eights = rows // ROW_BLOCK
    streams = next(s for s in (4, 3, 5, 2, 1) if eights % s == 0)
    block = (1,) + view.shape[1:]
    spec = lambda s: pl.BlockSpec(block, lambda i: (i * streams + s + first, 0, 0, 0, 0))
    return pl.pallas_call(
        prepare_kernel,
        grid=(eights // streams,),
        in_specs=[spec(s) for s in range(streams)],
        out_specs=pl.BlockSpec((streams * ROW_BLOCK, slow, N1), lambda i: (i, 0, 0)),
        out_shape=jax.ShapeDtypeStruct((rows, slow, N1), jnp.bfloat16),
        compiler_params=pltpu.CompilerParams(vmem_limit_bytes=VMEM_LIMIT),
        cost_estimate=pl.CostEstimate(
            flops=rows * slow * N1, bytes_accessed=rows * slow * N1 * 6, transcendentals=0
        ),
        name="prepare",
    )(*[view] * streams)


def spectrum_kernel(x_ref, table_ref, cos_ref, sin_ref, o_ref, *, block):
    parts, _, slow, _ = o_ref.shape
    data = x_ref[...].reshape(N2, N1)
    dot = functools.partial(jnp.dot, preferred_element_type=jnp.float32)
    for start in range(0, N2, block):
        rows = slice(start, start + block)
        real = dot(table_ref[rows, :], data)
        imag = dot(table_ref[N2 + start : N2 + start + block, :], data)
        cosine = cos_ref[rows, :]
        sine = sin_ref[rows, :]
        twisted_re = (real * cosine + imag * sine).astype(jnp.bfloat16)
        twisted_im = (imag * cosine - real * sine).astype(jnp.bfloat16)
        table_cos = table_ref[:N1, :HALF]
        minus_sin = table_ref[N1:, :HALF]
        bins_re = dot(twisted_re, table_cos) - dot(twisted_im, minus_sin)
        bins_im = dot(twisted_re, minus_sin) + dot(twisted_im, table_cos)
        feats = jnp.log(1.0 + (bins_re**2 + bins_im**2)).astype(jnp.bfloat16)
        if parts == 1:
            o_ref[0, 0, rows, :] = feats
        else:
            o_ref[start // slow : (start + block) // slow, 0] = feats.reshape(
                block // slow, slow, HALF
            )


def spectrum(blocks, consts):
    parts, count, slow, _ = blocks.shape
    whole = lambda a: pl.BlockSpec(a.shape, lambda i: (0, 0))
    return pl.pallas_call(
        functools.partial(spectrum_kernel, block=max(128, slow)),
        grid=(count,),
        in_specs=[pl.BlockSpec((parts, 1, slow, N1), lambda i: (0, i, 0, 0))]
        + [whole(a) for a in consts],
        out_specs=pl.BlockSpec((parts, 1, slow, HALF), lambda i: (0, i, 0, 0)),
        out_shape=jax.ShapeDtypeStruct((parts, count, slow, HALF), jnp.bfloat16),
        compiler_params=pltpu.CompilerParams(vmem_limit_bytes=VMEM_LIMIT),
        cost_estimate=pl.CostEstimate(
            flops=count * 8 * N1 * N2 * N2,
            bytes_accessed=count * N1 * N2 * 3 + 4 * 2**20,
            transcendentals=count * N2 * HALF,
        ),
        name="spectrum",
    )(blocks, *consts)


def gradient_kernel(*refs, block, slots):
    *feat_refs, dpre_ref, o_ref, buffer, sems = refs
    blocks = o_ref.shape[0] // block

    def copy(k):
        return pltpu.make_async_copy(
            buffer.at[k % slots], o_ref.at[pl.ds(k * block, block), :], sems.at[k % slots]
        )

    for k in range(blocks):
        if k >= slots:
            copy(k - slots).wait()
        feats = jnp.concatenate([ref[:, k * block : (k + 1) * block] for ref in feat_refs], 0)
        buffer[k % slots] = lax.dot_general(
            feats, dpre_ref[...], (((0,), (0,)), ((), ())), preferred_element_type=jnp.float32
        )
        copy(k).start()
    for k in range(max(0, blocks - slots), blocks):
        copy(k).wait()


def gradient(chunks, dpre):
    features, hid = chunks[0].shape[1], dpre.shape[1]
    block = min(256, features)
    slots = min(8, features // block)
    return pl.pallas_call(
        functools.partial(gradient_kernel, block=block, slots=slots),
        in_specs=[pl.BlockSpec(memory_space=pltpu.VMEM)] * (len(chunks) + 1),
        out_specs=pl.BlockSpec(memory_space=pl.ANY),
        out_shape=jax.ShapeDtypeStruct((features, hid), jnp.float32),
        scratch_shapes=[
            pltpu.VMEM((slots, block, hid), jnp.float32),
            pltpu.SemaphoreType.DMA((slots,)),
        ],
        compiler_params=pltpu.CompilerParams(vmem_limit_bytes=12 * 2**20),
        cost_estimate=pl.CostEstimate(
            flops=2 * features * hid * dpre.shape[0],
            bytes_accessed=features * hid * 4,
            transcendentals=0,
        ),
        name="gradient",
    )(*chunks, dpre)


def exchange(value, bit, devices):
    return lax.ppermute(value, "tm", [(i, i ^ bit) for i in range(devices)])


def product_kernel(feats_ref, weight_ref, o_ref, flat_ref, held_ref, sems, *, step):
    copies = []
    for k in range(weight_ref.shape[0] // step):
        span = pl.ds(k * step, step)
        copies.append(
            pltpu.make_async_copy(weight_ref.at[span, :], held_ref.at[span, :], sems.at[k])
        )
        copies[-1].start()
    if len(feats_ref.shape) == 3:
        rows, slow, width = feats_ref.shape
        for first in range(0, slow, 16):
            for start in range(0, rows, 16):
                for lane in range(0, width, LANES):
                    value = feats_ref[
                        start : start + 16, first : first + 16, lane : lane + LANES
                    ]
                    value = jnp.swapaxes(value, 0, 1)
                    for k in range(16):
                        column = (first + k) * width + lane
                        flat_ref[start : start + 16, column : column + LANES] = value[k]
    else:
        flat_ref[...] = feats_ref[...]
    total = None
    for k, copy in enumerate(copies):
        copy.wait()
        span = slice(k * step, (k + 1) * step)
        piece = jnp.dot(flat_ref[:, span], held_ref[span, :], preferred_element_type=jnp.float32)
        total = piece if total is None else total + piece
    o_ref[...] = total


def product(feats, weight):
    rows, (depth, hid) = feats.shape[0], weight.shape
    step = min(PRODUCT_STEP, depth)
    vmem = pl.BlockSpec(memory_space=pltpu.VMEM)
    return pl.pallas_call(
        functools.partial(product_kernel, step=step),
        in_specs=[vmem, pl.BlockSpec(memory_space=pl.ANY)],
        out_specs=[vmem, vmem],
        out_shape=[
            jax.ShapeDtypeStruct((rows, hid), jnp.float32),
            jax.ShapeDtypeStruct((rows, depth), feats.dtype),
        ],
        scratch_shapes=[
            pltpu.VMEM((depth, hid), weight.dtype),
            pltpu.SemaphoreType.DMA((depth // step,)),
        ],
        compiler_params=pltpu.CompilerParams(vmem_limit_bytes=49 * 2**20),
        cost_estimate=pl.CostEstimate(
            flops=2 * rows * weight.size, bytes_accessed=weight.size * 2, transcendentals=0
        ),
        name="product",
    )(feats, weight)


def sum_over(value, devices):
    quarter = value.shape[1] // 4
    if devices % 4:
        bit = 1
        while bit < devices:
            value = value + exchange(value, bit, devices)
            bit *= 2
        return value
    me = lax.axis_index("tm") % 4
    part = [
        lax.dynamic_slice_in_dim(value, (me ^ k) * quarter, quarter, 1) for k in range(4)
    ]
    got = [exchange(part[k], k, devices) for k in range(1, 4)]
    own = (part[0] + got[0]) + (got[1] + got[2])
    if devices == 16:
        got = [exchange(own, 4 * k, devices) for k in range(1, 4)]
        own = (own + got[0]) + (got[1] + got[2])
    else:
        bit = 4
        while bit < devices:
            own = own + exchange(own, bit, devices)
            bit *= 2
    got = [own] + [exchange(own, k, devices) for k in range(1, 4)]
    odd = (me % 2) == 1
    high = me >= 2
    low_pair = [jnp.where(odd, got[1], got[0]), jnp.where(odd, got[0], got[1])]
    high_pair = [jnp.where(odd, got[3], got[2]), jnp.where(odd, got[2], got[3])]
    return jnp.concatenate(
        [jnp.where(high, h, l) for l, h in zip(low_pair, high_pair)]
        + [jnp.where(high, l, h) for l, h in zip(low_pair, high_pair)],
        1,
    )


def on_device(records, labels, first_weight, first_bias, second_weight, second_bias):
    devices = lax.axis_size("tm")
    count, local = records.shape
    slow = local // N1
    each = count // devices
    chunks = {8: (3, 5)}.get(each, (each,))
    aligned = slow % 16 == 0
    consts = tables()
    pieces = N1 // LANES
    view = (
        records.reshape(count // ROW_BLOCK, ROW_BLOCK, slow, pieces, LANES)
        .transpose(0, 2, 3, 1, 4)
    )

    feature_chunks, pre_chunks = [], []
    row = 0
    for size in chunks:
        rows = size * devices
        if feature_chunks:
            view, *consts = lax.optimization_barrier((view, *consts))
        mine = prepare(view, row, rows, slow).reshape(devices, size, slow, N1)
        blocks = lax.all_to_all(mine, "tm", split_axis=0, concat_axis=0, tiled=True)
        if not aligned:
            blocks = blocks.transpose(1, 0, 2, 3).reshape(1, size, N2, N1)
        feats = spectrum(blocks, consts)
        if not aligned:
            feats = feats.reshape(size, devices, slow, HALF).transpose(1, 0, 2, 3)
        feats = lax.all_to_all(feats, "tm", split_axis=0, concat_axis=0, tiled=True)
        feats = feats.reshape((rows, slow, HALF) if aligned else (rows, slow * HALF))
        partial_sums, feats = product(feats, first_weight)
        feature_chunks.append(feats)
        pre_chunks.append(sum_over(partial_sums, devices))
        row += rows
    pre = jnp.concatenate(pre_chunks, 0) + first_bias[None, :]

    target = labels.astype(jnp.float32)
    gate = jax.nn.sigmoid(pre)
    hidden = pre * gate
    logit = jnp.sum(hidden * second_weight[None, :], 1) + second_bias[0]
    dlogit = jax.nn.sigmoid(logit) - target
    dpre = (dlogit[:, None] * second_weight[None, :] * gate * (1.0 + pre * (1.0 - gate))).astype(
        jnp.bfloat16
    )
    grad_first = gradient(feature_chunks, dpre)
    grad_bias = jnp.sum(dpre.astype(jnp.float32), 0)
    grad_second = jnp.sum(hidden * dlogit[:, None], 0)
    loss = jnp.mean(jnp.log(1.0 + jnp.exp(logit)) - target * logit).reshape(1)
    grad_out_bias = jnp.sum(dlogit).reshape(1)
    return (loss, grad_first, grad_bias, grad_second, grad_out_bias)


def solution(mesh):
    return jax.shard_map(
        on_device,
        mesh=mesh,
        in_specs=(P("group", "tm"), P("group"), P("tm", None), P(), P(), P()),
        out_specs=(P("group"), P(("group", "tm"), None), P("group"), P("group"), P("group")),
        check_vma=False,
    )
```

```python
import functools
import math

import jax
import jax.numpy as jnp
import numpy as np
from jax import lax
from jax.experimental import pallas as pl
from jax.experimental.pallas import tpu as pltpu
from jax.sharding import PartitionSpec as P

N1 = 512
N2 = 512
HALF = N1 // 2
LANES = 128
ROW_BLOCK = 8
VMEM_LIMIT = 50 * 2**20
PRODUCT_STEP = 512


def tables():
    rows = np.arange(N2)[:, None]
    cols = np.arange(N2)[None, :]
    angle = 2.0 * math.pi / N2 * (rows * cols % N2)
    scale = 1.0 / math.sqrt(N2)
    table = np.concatenate([np.cos(angle) * scale, -np.sin(angle) * scale], 0)
    total = N1 * N2
    slow = jnp.arange(N2, dtype=jnp.int32)[:, None]
    fast = jnp.arange(N1, dtype=jnp.int32)[None, :]
    phase = 2.0 * math.pi / total * (slow * fast % total).astype(jnp.float32)
    return jnp.asarray(table.astype(np.float32), jnp.bfloat16), jnp.cos(phase), jnp.sin(phase)


def prepare_kernel(*refs):
    *x_refs, o_ref = refs
    slow = o_ref.shape[1]
    step = math.gcd(slow, 16)
    for eight, x_ref in enumerate(x_refs):
        recs = slice(eight * ROW_BLOCK, (eight + 1) * ROW_BLOCK)
        for start in range(0, slow, step):
            rows = slice(start, start + step)
            for piece in range(N1 // LANES):
                value = x_ref[0, rows, piece].astype(jnp.bfloat16)
                o_ref[recs, rows, piece * LANES : (piece + 1) * LANES] = jnp.swapaxes(value, 0, 1)


def prepare(view, first_row, rows, slow):
    first = first_row // ROW_BLOCK
    eights = rows // ROW_BLOCK
    streams = next(s for s in (4, 3, 5, 2, 1) if eights % s == 0)
    block = (1,) + view.shape[1:]
    spec = lambda s: pl.BlockSpec(block, lambda i: (i * streams + s + first, 0, 0, 0, 0))
    return pl.pallas_call(
        prepare_kernel,
        grid=(eights // streams,),
        in_specs=[spec(s) for s in range(streams)],
        out_specs=pl.BlockSpec((streams * ROW_BLOCK, slow, N1), lambda i: (i, 0, 0)),
        out_shape=jax.ShapeDtypeStruct((rows, slow, N1), jnp.bfloat16),
        compiler_params=pltpu.CompilerParams(vmem_limit_bytes=VMEM_LIMIT),
        cost_estimate=pl.CostEstimate(
            flops=rows * slow * N1, bytes_accessed=rows * slow * N1 * 6, transcendentals=0
        ),
        name="prepare",
    )(*[view] * streams)


def spectrum_kernel(x_ref, table_ref, cos_ref, sin_ref, o_ref, *, block):
    parts, _, slow, _ = o_ref.shape
    data = x_ref[...].reshape(N2, N1)
    dot = functools.partial(jnp.dot, preferred_element_type=jnp.float32)
    for start in range(0, N2, block):
        rows = slice(start, start + block)
        real = dot(table_ref[rows, :], data)
        imag = dot(table_ref[N2 + start : N2 + start + block, :], data)
        cosine = cos_ref[rows, :]
        sine = sin_ref[rows, :]
        twisted_re = (real * cosine + imag * sine).astype(jnp.bfloat16)
        twisted_im = (imag * cosine - real * sine).astype(jnp.bfloat16)
        table_cos = table_ref[:N1, :HALF]
        minus_sin = table_ref[N1:, :HALF]
        bins_re = dot(twisted_re, table_cos) - dot(twisted_im, minus_sin)
        bins_im = dot(twisted_re, minus_sin) + dot(twisted_im, table_cos)
        feats = jnp.log(1.0 + (bins_re**2 + bins_im**2)).astype(jnp.bfloat16)
        if parts == 1:
            o_ref[0, 0, rows, :] = feats
        else:
            o_ref[start // slow : (start + block) // slow, 0] = feats.reshape(
                block // slow, slow, HALF
            )


def spectrum(blocks, consts):
    parts, count, slow, _ = blocks.shape
    whole = lambda a: pl.BlockSpec(a.shape, lambda i: (0, 0))
    return pl.pallas_call(
        functools.partial(spectrum_kernel, block=max(128, slow)),
        grid=(count,),
        in_specs=[pl.BlockSpec((parts, 1, slow, N1), lambda i: (0, i, 0, 0))]
        + [whole(a) for a in consts],
        out_specs=pl.BlockSpec((parts, 1, slow, HALF), lambda i: (0, i, 0, 0)),
        out_shape=jax.ShapeDtypeStruct((parts, count, slow, HALF), jnp.bfloat16),
        compiler_params=pltpu.CompilerParams(vmem_limit_bytes=VMEM_LIMIT),
        cost_estimate=pl.CostEstimate(
            flops=count * 8 * N1 * N2 * N2,
            bytes_accessed=count * N1 * N2 * 3 + 4 * 2**20,
            transcendentals=count * N2 * HALF,
        ),
        name="spectrum",
    )(blocks, *consts)


def gradient_kernel(*refs, block, slots):
    *feat_refs, dpre_ref, o_ref, buffer, sems = refs
    blocks = o_ref.shape[0] // block

    def copy(k):
        return pltpu.make_async_copy(
            buffer.at[k % slots], o_ref.at[pl.ds(k * block, block), :], sems.at[k % slots]
        )

    for k in range(blocks):
        if k >= slots:
            copy(k - slots).wait()
        feats = jnp.concatenate([ref[:, k * block : (k + 1) * block] for ref in feat_refs], 0)
        buffer[k % slots] = lax.dot_general(
            feats, dpre_ref[...], (((0,), (0,)), ((), ())), preferred_element_type=jnp.float32
        )
        copy(k).start()
    for k in range(max(0, blocks - slots), blocks):
        copy(k).wait()


def gradient(chunks, dpre):
    features, hid = chunks[0].shape[1], dpre.shape[1]
    block = min(256, features)
    slots = min(8, features // block)
    return pl.pallas_call(
        functools.partial(gradient_kernel, block=block, slots=slots),
        in_specs=[pl.BlockSpec(memory_space=pltpu.VMEM)] * (len(chunks) + 1),
        out_specs=pl.BlockSpec(memory_space=pl.ANY),
        out_shape=jax.ShapeDtypeStruct((features, hid), jnp.float32),
        scratch_shapes=[
            pltpu.VMEM((slots, block, hid), jnp.float32),
            pltpu.SemaphoreType.DMA((slots,)),
        ],
        compiler_params=pltpu.CompilerParams(vmem_limit_bytes=12 * 2**20),
        cost_estimate=pl.CostEstimate(
            flops=2 * features * hid * dpre.shape[0],
            bytes_accessed=features * hid * 4,
            transcendentals=0,
        ),
        name="gradient",
    )(*chunks, dpre)


def exchange(value, bit, devices):
    return lax.ppermute(value, "tm", [(i, i ^ bit) for i in range(devices)])


def product_kernel(feats_ref, weight_ref, o_ref, flat_ref, held_ref, sems, *, step):
    copies = []
    for k in range(weight_ref.shape[0] // step):
        span = pl.ds(k * step, step)
        copies.append(
            pltpu.make_async_copy(weight_ref.at[span, :], held_ref.at[span, :], sems.at[k])
        )
        copies[-1].start()
    if len(feats_ref.shape) == 3:
        rows, slow, width = feats_ref.shape
        for first in range(0, slow, 16):
            for start in range(0, rows, 16):
                for lane in range(0, width, LANES):
                    value = feats_ref[
                        start : start + 16, first : first + 16, lane : lane + LANES
                    ]
                    value = jnp.swapaxes(value, 0, 1)
                    for k in range(16):
                        column = (first + k) * width + lane
                        flat_ref[start : start + 16, column : column + LANES] = value[k]
    else:
        flat_ref[...] = feats_ref[...]
    total = None
    for k, copy in enumerate(copies):
        copy.wait()
        span = slice(k * step, (k + 1) * step)
        piece = jnp.dot(flat_ref[:, span], held_ref[span, :], preferred_element_type=jnp.float32)
        total = piece if total is None else total + piece
    o_ref[...] = total


def product(feats, weight):
    rows, (depth, hid) = feats.shape[0], weight.shape
    step = min(PRODUCT_STEP, depth)
    vmem = pl.BlockSpec(memory_space=pltpu.VMEM)
    return pl.pallas_call(
        functools.partial(product_kernel, step=step),
        in_specs=[vmem, pl.BlockSpec(memory_space=pl.ANY)],
        out_specs=[vmem, vmem],
        out_shape=[
            jax.ShapeDtypeStruct((rows, hid), jnp.float32),
            jax.ShapeDtypeStruct((rows, depth), feats.dtype),
        ],
        scratch_shapes=[
            pltpu.VMEM((depth, hid), weight.dtype),
            pltpu.SemaphoreType.DMA((depth // step,)),
        ],
        compiler_params=pltpu.CompilerParams(vmem_limit_bytes=49 * 2**20),
        cost_estimate=pl.CostEstimate(
            flops=2 * rows * weight.size, bytes_accessed=weight.size * 2, transcendentals=0
        ),
        name="product",
    )(feats, weight)


def sum_over(value, devices):
    quarter = value.shape[1] // 4
    if devices % 4:
        bit = 1
        while bit < devices:
            value = value + exchange(value, bit, devices)
            bit *= 2
        return value
    me = lax.axis_index("tm") % 4
    part = [
        lax.dynamic_slice_in_dim(value, (me ^ k) * quarter, quarter, 1) for k in range(4)
    ]
    got = [exchange(part[k], k, devices) for k in range(1, 4)]
    own = (part[0] + got[0]) + (got[1] + got[2])
    if devices == 16:
        got = [exchange(own, 4 * k, devices) for k in range(1, 4)]
        own = (own + got[0]) + (got[1] + got[2])
    else:
        bit = 4
        while bit < devices:
            own = own + exchange(own, bit, devices)
            bit *= 2
    own = lax.reduce_precision(own, 8, 7).astype(jnp.bfloat16)
    got = [own] + [exchange(own, k, devices) for k in range(1, 4)]
    got = [part.astype(jnp.float32) for part in got]
    odd = (me % 2) == 1
    high = me >= 2
    low_pair = [jnp.where(odd, got[1], got[0]), jnp.where(odd, got[0], got[1])]
    high_pair = [jnp.where(odd, got[3], got[2]), jnp.where(odd, got[2], got[3])]
    return jnp.concatenate(
        [jnp.where(high, h, l) for l, h in zip(low_pair, high_pair)]
        + [jnp.where(high, l, h) for l, h in zip(low_pair, high_pair)],
        1,
    )


def on_device(records, labels, first_weight, first_bias, second_weight, second_bias):
    devices = lax.axis_size("tm")
    count, local = records.shape
    slow = local // N1
    each = count // devices
    chunks = {8: (3, 5)}.get(each, (each,))
    aligned = slow % 16 == 0
    consts = tables()
    pieces = N1 // LANES
    view = (
        records.reshape(count // ROW_BLOCK, ROW_BLOCK, slow, pieces, LANES)
        .transpose(0, 2, 3, 1, 4)
    )

    feature_chunks, pre_chunks = [], []
    row = 0
    for size in chunks:
        rows = size * devices
        if feature_chunks:
            view, *consts = lax.optimization_barrier((view, *consts))
        mine = prepare(view, row, rows, slow).reshape(devices, size, slow, N1)
        blocks = lax.all_to_all(mine, "tm", split_axis=0, concat_axis=0, tiled=True)
        if not aligned:
            blocks = blocks.transpose(1, 0, 2, 3).reshape(1, size, N2, N1)
        feats = spectrum(blocks, consts)
        if not aligned:
            feats = feats.reshape(size, devices, slow, HALF).transpose(1, 0, 2, 3)
        feats = lax.all_to_all(feats, "tm", split_axis=0, concat_axis=0, tiled=True)
        feats = feats.reshape((rows, slow, HALF) if aligned else (rows, slow * HALF))
        partial_sums, feats = product(feats, first_weight)
        feature_chunks.append(feats)
        pre_chunks.append(sum_over(partial_sums, devices))
        row += rows
    pre = jnp.concatenate(pre_chunks, 0) + first_bias[None, :]

    target = labels.astype(jnp.float32)
    gate = jax.nn.sigmoid(pre)
    hidden = pre * gate
    logit = jnp.sum(hidden * second_weight[None, :], 1) + second_bias[0]
    dlogit = jax.nn.sigmoid(logit) - target
    dpre = (dlogit[:, None] * second_weight[None, :] * gate * (1.0 + pre * (1.0 - gate))).astype(
        jnp.bfloat16
    )
    grad_first = gradient(feature_chunks, dpre)
    grad_bias = jnp.sum(dpre.astype(jnp.float32), 0)
    grad_second = jnp.sum(hidden * dlogit[:, None], 0)
    loss = jnp.mean(jnp.log(1.0 + jnp.exp(logit)) - target * logit).reshape(1)
    grad_out_bias = jnp.sum(dlogit).reshape(1)
    return (loss, grad_first, grad_bias, grad_second, grad_out_bias)


def solution(mesh):
    return jax.shard_map(
        on_device,
        mesh=mesh,
        in_specs=(P("group", "tm"), P("group"), P("tm", None), P(), P(), P()),
        out_specs=(P("group"), P(("group", "tm"), None), P("group"), P("group"), P("group")),
        check_vma=False,
    )
```
